32 devices in a mesh: clips: 2 (over y), sa: 4 (over z), wa: 2 (over x), hp: 2 (over core).
Axes of the slice: x: 2, y: 2, z: 4, core: 2. Of those that a mesh axis runs over, the one named last changes fastest.
Arguments:
- queries: bfloat16 [16, 8, 16, 3072], P(('clips', 'sa'), None, 'wa', 'hp'), parts along dimension 0, may hold values from -6 to 6
- keys: bfloat16 [16, 8, 16, 3072], P(('clips', 'sa'), None, 'wa', 'hp'), parts along dimension 0, may hold values from -6 to 6
- values: bfloat16 [16, 8, 16, 3072], P(('clips', 'sa'), None, 'wa', 'hp'), parts along dimension 0, may hold values from -6 to 6
- text_keys: bfloat16 [512, 3072], P(('clips', 'sa'), 'hp'), parts along dimension 0, may hold values from -6 to 6
- text_values: bfloat16 [512, 3072], P(('clips', 'sa'), 'hp'), parts along dimension 0, may hold values from -6 to 6
- out_grad: bfloat16 [16, 8, 16, 3072], P(('clips', 'sa'), None, 'wa', 'hp'), parts along dimension 0, may hold values from -6 to 6
- window_ext: int32 [24, 3], P('hp'), may hold values from 0 to 1, as said below
Outputs:
- attended: bfloat16 [16, 8, 16, 3072], P(('clips', 'sa'), None, 'wa', 'hp'), parts along dimension 0
- query_grad: bfloat16 [16, 8, 16, 3072], P(('clips', 'sa'), None, 'wa', 'hp'), parts along dimension 0
- key_grad: bfloat16 [16, 8, 16, 3072], P(('clips', 'sa'), None, 'wa', 'hp'), parts along dimension 0
- value_grad: bfloat16 [16, 8, 16, 3072], P(('clips', 'sa'), None, 'wa', 'hp'), parts along dimension 0
- text_key_grad: float32 [512, 3072], P(('clips', 'sa'), 'hp'), parts along dimension 0
- text_value_grad: float32 [512, 3072], P(('clips', 'sa'), 'hp'), parts along dimension 0
The draws below stay inside these ranges and needn't reach their ends.
There are 2 independent parts, one for each index of `clips`. The reference program is written for one: setup_inputs(seed, part) draws one part's arguments, and reference() takes and returns one part's arrays. A program takes and returns all parts, laid end to end along the dimension named above; an argument that names none is the same for every part. Nothing has to cross between parts.
Inputs may be any that keep to these rules, and one draw needn't show every extreme that they name: `window_ext`: columns 0, 1 and 2 are at most 1, 1 and 1; each of these bounds is reached by some head.
All inputs are finite; a program needn't handle non-finite values.
Results may differ from the reference program's by a relative error of at most 0.012.
The reference program's roundings to bfloat16 on the way count: a program that leaves them out, or rounds other values in their place, can miss the bound.
Values may be sent and summed in bfloat16 or wider, within the bound.
A program may use at most 128 MiB of HBM per device.

```python
import jax
import jax.numpy as jnp
from jax import lax

HEADS = 24
HEAD_DIM = 128
TEXT_TOKENS = 256
FRAMES_DEV = 2
HEIGHT = 8
COLS_DEV = 8
TILE_T = 2
TILE_H = 8
TILE_W = 8
EXT_T = 1
EXT_H = 1
EXT_W = 1
FRAMES = 8
WIDTH = 16
N_SA = 4
N_WA = 2


def draw_queries(key, part):
    full_shape = (FRAMES, HEIGHT, WIDTH, HEADS * HEAD_DIM)
    result = jax.random.truncated_normal(jax.random.fold_in(key, 1), -6.0, 6.0, full_shape, jnp.float32)
    return result.astype(jnp.bfloat16)


def draw_keys(key, part):
    full_shape = (FRAMES, HEIGHT, WIDTH, HEADS * HEAD_DIM)
    result = jax.random.truncated_normal(jax.random.fold_in(key, 2), -6.0, 6.0, full_shape, jnp.float32)
    return result.astype(jnp.bfloat16)


def draw_window_ext(key, part):
    columns_out = []
    bounds = (EXT_T, EXT_H, EXT_W)
    for axis_number in range(3):
        drawn = jax.random.randint(jax.random.fold_in(key, 20 + axis_number), (HEADS,), 0, bounds[axis_number] + 1)
        chosen = jax.random.randint(jax.random.fold_in(key, 30 + axis_number), (), 0, HEADS)
        drawn = jnp.where(jnp.arange(HEADS, dtype=jnp.int32) == chosen, bounds[axis_number], drawn)
        columns_out.append(drawn.astype(jnp.int32))
    return jnp.stack(columns_out, axis=1)


def level_of(stream_key, shape, pieces, low, largest):
    factor_of, own = 1.0, jax.random.fold_in(stream_key, 6)
    for position, shards_of in pieces:
        steps = jnp.exp(jax.random.uniform(jax.random.fold_in(own, position), (shards_of,), jnp.float32, low / len(pieces), largest / len(pieces)))
        factor_of = factor_of * jnp.repeat(steps, shape[position] // shards_of).reshape([-1 if axis == position else 1 for axis in range(len(shape))])
    return factor_of


def gaussian(stream_key, dims, scale, reach, shards=(), held_as=jnp.bfloat16):
    level = level_of(stream_key, dims, shards, -0.22, 0.18) if shards else 1.0
    values = jax.random.normal(stream_key, dims, jnp.float32) * scale * level
    return jnp.minimum(jnp.maximum(values, -reach), reach).astype(held_as)


def setup_inputs(seed: int = 0, part: int = 0) -> dict:
    key_of = jax.random.split(jax.random.key(seed), 8)
    part_splits = jax.random.split(jax.random.fold_in(key_of[7], part), 8)
    return {
        "queries": draw_queries(jax.random.fold_in(jax.random.fold_in(key_of[7], part), 71), part),
        "keys": draw_keys(jax.random.fold_in(jax.random.fold_in(key_of[7], part), 71), part),
        "values": gaussian(part_splits[2], (FRAMES, HEIGHT, WIDTH, HEADS * HEAD_DIM), 1.0, 6.0, ((0, 4), (2, 2), (3, 2))),
        "text_keys": gaussian(part_splits[3], (TEXT_TOKENS, HEADS * HEAD_DIM), 1.0, 6.0, ((0, 4), (1, 2))),
        "text_values": gaussian(part_splits[4], (TEXT_TOKENS, HEADS * HEAD_DIM), 1.0, 6.0, ((0, 4), (1, 2))),
        "out_grad": gaussian(part_splits[5], (FRAMES, HEIGHT, WIDTH, HEADS * HEAD_DIM), 1.0, 6.0, ((0, 4), (2, 2), (3, 2))),
        "window_ext": draw_window_ext(jax.random.fold_in(key_of[7], 71), part),
    }


def tile_coords(time_start, frame_count, row_count, col_start, col_count, total_frames, total_cols):
    times = time_start + jnp.arange(frame_count, dtype=jnp.int32)
    heights = jnp.arange(row_count, dtype=jnp.int32)
    columns = col_start + jnp.arange(col_count, dtype=jnp.int32)
    grid_shape = (frame_count, row_count, col_count)
    time_grid = jnp.broadcast_to(times[:, None, None], grid_shape).reshape(-1)
    height_grid = jnp.broadcast_to(heights[None, :, None], grid_shape).reshape(-1)
    col_grid = jnp.broadcast_to(columns[None, None, :], grid_shape).reshape(-1)
    inside = (time_grid >= 0) & (time_grid < total_frames) & (col_grid >= 0) & (col_grid < total_cols)
    return (time_grid // TILE_T, height_grid // TILE_H, col_grid // TILE_W, inside)


def pair_mask(first, second, window):
    allowed = first[3][:, None] & second[3][None, :]
    for axis_number in range(3):
        apart = jnp.abs(first[axis_number][:, None] - second[axis_number][None, :])
        allowed = allowed & (apart <= window[axis_number])
    return allowed


def forward_head(query_head, key_head, value_head, text_key, text_value, allowed):
    score_scale = HEAD_DIM ** -0.5
    video_scores = jnp.dot(query_head, key_head.T, preferred_element_type=jnp.float32) * score_scale
    video_scores = jnp.where(allowed, video_scores, -1e30)
    text_scores = jnp.dot(query_head, text_key.T, preferred_element_type=jnp.float32) * score_scale
    row_max = jnp.maximum(jnp.max(video_scores, axis=1), jnp.max(text_scores, axis=1))
    denom_sum = jnp.sum(jnp.exp(video_scores - row_max[:, None]), axis=1) + jnp.sum(jnp.exp(text_scores - row_max[:, None]), axis=1)
    log_total = row_max + jnp.log(denom_sum)
    video_weights = jnp.exp(video_scores - log_total[:, None]).astype(jnp.bfloat16)
    text_weights = jnp.exp(text_scores - log_total[:, None]).astype(jnp.bfloat16)
    attended_head = jnp.dot(video_weights, value_head, preferred_element_type=jnp.float32)
    attended_head = attended_head + jnp.dot(text_weights, text_value, preferred_element_type=jnp.float32)
    return attended_head.astype(jnp.bfloat16), log_total


def grads_head(query_head, grad_head, log_total, row_delta, key_head, value_head, text_key, text_value, allowed):
    score_scale = HEAD_DIM ** -0.5
    video_scores = jnp.dot(query_head, key_head.T, preferred_element_type=jnp.float32) * score_scale
    video_scores = jnp.where(allowed, video_scores, -1e30)
    text_scores = jnp.dot(query_head, text_key.T, preferred_element_type=jnp.float32) * score_scale
    video_probs = jnp.exp(video_scores - log_total[:, None])
    text_probs = jnp.exp(text_scores - log_total[:, None])
    video_dprobs = jnp.dot(grad_head, value_head.T, preferred_element_type=jnp.float32)
    text_dprobs = jnp.dot(grad_head, text_value.T, preferred_element_type=jnp.float32)
    video_dscores = (video_probs * (video_dprobs - row_delta[:, None]) * score_scale).astype(jnp.bfloat16)
    text_dscores = (text_probs * (text_dprobs - row_delta[:, None]) * score_scale).astype(jnp.bfloat16)
    query_term = jnp.dot(video_dscores, key_head, preferred_element_type=jnp.float32)
    query_term = query_term + jnp.dot(text_dscores, text_key, preferred_element_type=jnp.float32)
    key_term = jnp.dot(video_dscores.T, query_head, preferred_element_type=jnp.float32)
    value_term = jnp.dot(video_probs.astype(jnp.bfloat16).T, grad_head, preferred_element_type=jnp.float32)
    text_key_term = jnp.dot(text_dscores.T, query_head, preferred_element_type=jnp.float32)
    text_value_term = jnp.dot(text_probs.astype(jnp.bfloat16).T, grad_head, preferred_element_type=jnp.float32)
    return query_term, key_term, value_term, text_key_term, text_value_term


def reference(queries, keys, values, text_keys, text_values, out_grad, window_ext):
    rim_time = EXT_T * TILE_T
    rim_cols = EXT_W * TILE_W
    near_shape = (FRAMES_DEV + 2 * rim_time, HEIGHT, COLS_DEV + 2 * rim_cols, HEAD_DIM)
    own_shape = (FRAMES_DEV, HEIGHT, COLS_DEV, HEAD_DIM)

    def heads_first(tensor):
        return jnp.moveaxis(tensor.reshape(FRAMES, HEIGHT, WIDTH, HEADS, HEAD_DIM), 3, 0)

    def text_first(tensor):
        return jnp.moveaxis(tensor.reshape(TEXT_TOKENS, HEADS, HEAD_DIM), 1, 0)

    def one_head(operands):
        query_all, key_all, value_all, grad_all, text_key, text_value, window = operands
        padding = ((rim_time, rim_time), (0, 0), (rim_cols, rim_cols), (0, 0))
        key_padded = jnp.pad(key_all, padding)
        value_padded = jnp.pad(value_all, padding)

        def block(running, block_index):
            key_acc, value_acc, text_key_acc, text_value_acc = running
            time_start = (block_index // N_WA) * FRAMES_DEV
            col_start = (block_index % N_WA) * COLS_DEV
            corner = (time_start, jnp.int32(0), col_start, jnp.int32(0))
            query_block = lax.dynamic_slice(query_all, corner, own_shape).reshape(-1, HEAD_DIM)
            grad_block = lax.dynamic_slice(grad_all, corner, own_shape).reshape(-1, HEAD_DIM)
            key_block = lax.dynamic_slice(key_padded, corner, near_shape).reshape(-1, HEAD_DIM)
            value_block = lax.dynamic_slice(value_padded, corner, near_shape).reshape(-1, HEAD_DIM)
            own_cells = tile_coords(time_start, FRAMES_DEV, HEIGHT, col_start, COLS_DEV, FRAMES, WIDTH)
            near_cells = tile_coords(time_start - rim_time, FRAMES_DEV + 2 * rim_time, HEIGHT, col_start - rim_cols, COLS_DEV + 2 * rim_cols, FRAMES, WIDTH)
            allowed = pair_mask(own_cells, near_cells, window)
            attended_head, log_total = forward_head(query_block, key_block, value_block, text_key, text_value, allowed)
            row_delta = jnp.sum(grad_block.astype(jnp.float32) * attended_head.astype(jnp.float32), axis=1)
            query_term, key_term, value_term, text_key_term, text_value_term = grads_head(query_block, grad_block, log_total, row_delta, key_block, value_block, text_key, text_value, allowed)
            key_acc = lax.dynamic_update_slice(key_acc, lax.dynamic_slice(key_acc, corner, near_shape) + key_term.reshape(near_shape), corner)
            value_acc = lax.dynamic_update_slice(value_acc, lax.dynamic_slice(value_acc, corner, near_shape) + value_term.reshape(near_shape), corner)
            running = (key_acc, value_acc, text_key_acc + text_key_term, text_value_acc + text_value_term)
            return running, (attended_head.reshape(own_shape), query_term.astype(jnp.bfloat16).reshape(own_shape))

        padded_shape = (FRAMES + 2 * rim_time, HEIGHT, WIDTH + 2 * rim_cols, HEAD_DIM)
        start = (jnp.zeros(padded_shape, jnp.float32), jnp.zeros(padded_shape, jnp.float32), jnp.zeros((TEXT_TOKENS, HEAD_DIM), jnp.float32), jnp.zeros((TEXT_TOKENS, HEAD_DIM), jnp.float32))
        running, stacked = lax.scan(block, start, jnp.arange(N_SA * N_WA, dtype=jnp.int32))

        def regrid(blocks):
            blocks = blocks.reshape(N_SA, N_WA, FRAMES_DEV, HEIGHT, COLS_DEV, HEAD_DIM)
            return jnp.transpose(blocks, (0, 2, 3, 1, 4, 5)).reshape(FRAMES, HEIGHT, WIDTH, HEAD_DIM)

        key_grad_head = running[0][rim_time:rim_time + FRAMES, :, rim_cols:rim_cols + WIDTH].astype(jnp.bfloat16)
        value_grad_head = running[1][rim_time:rim_time + FRAMES, :, rim_cols:rim_cols + WIDTH].astype(jnp.bfloat16)
        return regrid(stacked[0]), regrid(stacked[1]), key_grad_head, value_grad_head, running[2], running[3]

    results = lax.map(one_head, (heads_first(queries), heads_first(keys), heads_first(values), heads_first(out_grad), text_first(text_keys), text_first(text_values), window_ext))

    def grid_back(tensor):
        return jnp.moveaxis(tensor, 0, 3).reshape(FRAMES, HEIGHT, WIDTH, HEADS * HEAD_DIM)

    def text_back(tensor):
        return jnp.moveaxis(tensor, 0, 1).reshape(TEXT_TOKENS, HEADS * HEAD_DIM)

    return (grid_back(results[0]), grid_back(results[1]), grid_back(results[2]), grid_back(results[3]), text_back(results[4]), text_back(results[5]))
```

```python
import functools

import jax
import jax.numpy as jnp
from jax import lax
from jax.experimental import pallas as pl
from jax.experimental.pallas import tpu as pltpu
from jax.sharding import PartitionSpec as P

HEAD_DIM = 128
NEG = -1e30
MESH = pl.DeviceIdType.MESH
F32 = jnp.float32
BF16 = jnp.bfloat16
KEY_BLOCK = 256
LOOKAHEAD = 2
LAG = 2


def dot_nt(a, b):
    return lax.dot_general(a, b, (((1,), (1,)), ((), ())), preferred_element_type=F32)


def dot_tn(a, b):
    return lax.dot_general(a, b, (((0,), (0,)), ((), ())), preferred_element_type=F32)


def kernel(
    n_sa, n_wa, heads, cells, text_rows,
    window, q_in, k_in, v_in, g_in, tk_in, tv_in,
    o_out, dq_out, dk_out, dv_out, dtk_out, dtv_out,
    kv, qg, oq, own_part, z_part, z_got, fin, t_part, t_got, t_fin, st, wb, db,
    x_send, x_recv, x_loc, t_send, t_recv, t_loc, z_send, z_recv,
    r_send, r_recv, y_send, y_recv, y_loc, g_send, g_recv, f_send, f_recv,
):
    s = lax.axis_index("sa")
    w = lax.axis_index("wa")
    slab = n_wa * cells
    text = n_sa * text_rows
    text_base = 3 * slab
    n_keys = text_base + text
    scale = HEAD_DIM ** (-0.5)
    has_prev, has_next = s > 0, s < n_sa - 1

    def cols(group, h):
        return pl.ds(pl.multiple_of((group * heads + h) * HEAD_DIM, HEAD_DIM), HEAD_DIM)

    def rows_of(base, index, size):
        return pl.ds(pl.multiple_of(base + index * size, 16), size)

    def remote(src, dst, send, recv, **where):
        return pltpu.make_async_remote_copy(
            src_ref=src, dst_ref=dst, send_sem=send, recv_sem=recv,
            device_id=where, device_id_type=MESH,
        )

    barrier = pltpu.get_barrier_semaphore()
    for d in range(1, n_wa):
        pl.semaphore_signal(barrier, inc=1, device_id={"wa": lax.rem(w + d, n_wa)}, device_id_type=MESH)
    for e in range(1, n_sa):
        pl.semaphore_signal(barrier, inc=1, device_id={"sa": lax.rem(s + e, n_sa)}, device_id_type=MESH)
    pl.semaphore_wait(barrier, n_wa + n_sa - 2)

    ins = (k_in, v_in, q_in, g_in)

    def x_slot(kind, h, source):
        if kind < 2:
            return kv.at[h, kind, rows_of(slab, source, cells)]
        return qg.at[h, kind - 2, rows_of(0, source, cells)]

    def x_copy(kind, h, d, source):
        peer = lax.rem(w + d, n_wa)
        return remote(
            ins[kind].at[:, cols(peer, h)], x_slot(kind, h, source),
            x_send.at[d - 1, h, kind], x_recv.at[d - 1, h, kind], wa=peer,
        )

    def x_local(kind, h):
        return pltpu.make_async_copy(ins[kind].at[:, cols(w, h)], x_slot(kind, h, w), x_loc.at[h, kind])

    def x_wait(kind, h):
        x_local(kind, h).wait()
        for d in range(1, n_wa):
            x_copy(kind, h, d, lax.rem(w + n_wa - d, n_wa)).wait_recv()

    texts = (tk_in, tv_in)

    def t_slot(kind, h, source):
        return kv.at[h, kind, rows_of(text_base, source, text_rows)]

    def t_copy(kind, h, e, source):
        return remote(
            texts[kind].at[:, cols(w, h)], t_slot(kind, h, source),
            t_send.at[e - 1, h, kind], t_recv.at[e - 1, h, kind], sa=lax.rem(s + e, n_sa),
        )

    def t_local(kind, h):
        return pltpu.make_async_copy(texts[kind].at[:, cols(w, h)], t_slot(kind, h, s), t_loc.at[h, kind])

    def z_copy(side, h):
        target = lax.rem(s + 1, n_sa) if side == 0 else lax.rem(s + n_sa - 1, n_sa)
        return remote(
            kv.at[h, :, pl.ds(slab, slab)], kv.at[h, :, pl.ds(0 if side == 0 else 2 * slab, slab)],
            z_send.at[side, h], z_recv.at[side, h], sa=target,
        )

    def r_copy(side, h):
        target = lax.rem(s + n_sa - 1, n_sa) if side == 0 else lax.rem(s + 1, n_sa)
        return remote(
            z_part.at[side, h], z_got.at[side, h], r_send.at[side, h], r_recv.at[side, h], sa=target,
        )

    @pl.when(jnp.logical_not(has_prev))
    def _():
        def clear(h, c):
            kv[h, :, pl.ds(0, slab)] = jnp.zeros((2, slab, HEAD_DIM), BF16)
            z_got[1, h] = jnp.zeros((2, slab, HEAD_DIM), BF16)
            return c

        lax.fori_loop(0, heads, clear, 0)

    @pl.when(jnp.logical_not(has_next))
    def _():
        def clear(h, c):
            kv[h, :, pl.ds(2 * slab, slab)] = jnp.zeros((2, slab, HEAD_DIM), BF16)
            z_got[0, h] = jnp.zeros((2, slab, HEAD_DIM), BF16)
            return c

        lax.fori_loop(0, heads, clear, 0)

    def open_head(h, c):
        for kind in range(4):
            for d in range(1, n_wa):
                x_copy(kind, h, d, w).start()
            x_local(kind, h).start()
        return c

    lax.fori_loop(0, heads, open_head, 0)

    def feed(h):
        for kind in range(2):
            for e in range(1, n_sa):
                t_copy(kind, h, e, s).start()
            t_local(kind, h).start()
        x_wait(0, h)
        x_wait(1, h)

        @pl.when(has_next)
        def _():
            z_copy(0, h).start()

        @pl.when(has_prev)
        def _():
            z_copy(1, h).start()

    for h in range(min(LOOKAHEAD, heads)):
        feed(h)

    q_block = min(slab, 256)

    def compute(h):
        ext_t = window[w * heads + h, 0]
        ext_w = window[w * heads + h, 2]
        near = (
            jnp.logical_and(has_prev, ext_t >= 1),
            None,
            jnp.logical_and(has_next, ext_t >= 1),
        )
        for qb in range(slab // q_block):
            q_rows = pl.ds(qb * q_block, q_block)
            q = qg[h, 0, q_rows]
            g = qg[h, 1, q_rows]
            query_col = qb * (q_block // cells) + lax.broadcasted_iota(jnp.int32, (1, q_block), 1) // cells
            top = jnp.full((1, q_block), NEG, F32)
            blocks = []
            for j in range(3):
                far = 0.0 if near[j] is None else jnp.where(near[j], 0.0, NEG)
                for c in range(n_wa):
                    bias = jnp.where(jnp.abs(query_col - c) <= ext_w, far, NEG)
                    blocks.append(((j * n_wa + c) * cells, cells, bias))
            for b in range(0, text, KEY_BLOCK):
                blocks.append((text_base + b, min(KEY_BLOCK, text - b), None))
            for start, size, bias in blocks:
                sc = dot_nt(kv[h, 0, pl.ds(start, size)], q) * scale
                if bias is not None:
                    sc = sc + bias
                st[pl.ds(start, size)] = sc
                top = jnp.maximum(top, jnp.max(sc, axis=0, keepdims=True))
            total = jnp.zeros((1, q_block), F32)
            for start, size, _ in blocks:
                p = jnp.exp(st[pl.ds(start, size)] - top)
                st[pl.ds(start, size)] = p
                total = total + jnp.sum(p, axis=0, keepdims=True)
            inv = 1.0 / total
            for start, size, _ in blocks:
                wb[pl.ds(start, size)] = (st[pl.ds(start, size)] * inv).astype(BF16)
            attended = dot_tn(wb[...], kv[h, 1]).astype(BF16)
            oq[h, 0, q_rows] = attended
            product = g.astype(F32) * attended.astype(F32)
            delta = jnp.sum(product.T, axis=0, keepdims=True)
            inv_scale = inv * scale
            for start, size, _ in blocks:
                dp = dot_nt(kv[h, 1, pl.ds(start, size)], g)
                db[pl.ds(start, size)] = (st[pl.ds(start, size)] * inv_scale * (dp - delta)).astype(BF16)
            oq[h, 1, q_rows] = dot_tn(db[...], kv[h, 0]).astype(BF16)

            def put(ref, index, value, at):
                if qb == 0:
                    ref[index] = value.astype(ref.dtype)
                else:
                    ref[index] = (ref[index].astype(F32) + value).astype(ref.dtype)

            for kind, (left, right) in enumerate(((db, q), (wb, g))):
                for j in range(3):
                    part = jnp.dot(left[pl.ds(j * slab, slab)], right, preferred_element_type=F32)
                    if j == 1:
                        put(own_part, (h, kind), part, qb)
                    else:
                        put(z_part, (j // 2, h, kind), part, qb)
                part = jnp.dot(left[pl.ds(text_base, text)], right, preferred_element_type=F32)
                put(t_part, (h, kind), part, qb)

    outs = (dk_out, dv_out, o_out, dq_out)

    def y_src(kind, h, owner):
        ref = fin if kind < 2 else oq
        return ref.at[h, kind % 2, rows_of(0, owner, cells)]

    def y_copy(kind, h, d, source):
        peer = lax.rem(w + d, n_wa)
        return remote(
            y_src(kind, h, peer), outs[kind].at[:, cols(source, h)],
            y_send.at[d - 1, h, kind], y_recv.at[d - 1, h, kind], wa=peer,
        )

    def y_local(kind, h):
        return pltpu.make_async_copy(y_src(kind, h, w), outs[kind].at[:, cols(w, h)], y_loc.at[h, kind])

    def y_start(kind, h):
        for d in range(1, n_wa):
            y_copy(kind, h, d, w).start()
        y_local(kind, h).start()

    def g_copy(h, e):
        peer = lax.rem(s + e, n_sa)
        return remote(
            t_part.at[h, :, rows_of(0, peer, text_rows)], t_got.at[e - 1, h],
            g_send.at[e - 1, h], g_recv.at[e - 1, h], sa=peer,
        )

    def f_copy(h, d, source):
        return remote(
            t_fin.at[w, h], t_fin.at[source, h],
            f_send.at[d - 1, h], f_recv.at[d - 1, h], wa=lax.rem(w + d, n_wa),
        )

    def finish(h):
        @pl.when(has_next)
        def _():
            r_copy(0, h).wait_recv()

        @pl.when(has_prev)
        def _():
            r_copy(1, h).wait_recv()

        whole = own_part[h] + z_got[0, h].astype(F32) + z_got[1, h].astype(F32)
        fin[h] = whole.astype(BF16)
        y_start(0, h)
        y_start(1, h)
        whole = t_part[h, :, rows_of(0, s, text_rows)].astype(F32)
        for e in range(1, n_sa):
            g_copy(h, e).wait_recv()
            whole = whole + t_got[e - 1, h].astype(F32)
        t_fin[w, h] = whole.astype(BF16)
        for d in range(1, n_wa):
            f_copy(h, d, w).start()

    def step(h, c):
        @pl.when(h + LOOKAHEAD < heads)
        def _():
            feed(h + LOOKAHEAD)

        x_wait(2, h)
        x_wait(3, h)
        for kind in range(2):
            t_local(kind, h).wait()
            for e in range(1, n_sa):
                t_copy(kind, h, e, lax.rem(s + n_sa - e, n_sa)).wait_recv()

        @pl.when(has_prev)
        def _():
            z_copy(0, h).wait_recv()

        @pl.when(has_next)
        def _():
            z_copy(1, h).wait_recv()

        compute(h)

        @pl.when(has_prev)
        def _():
            r_copy(0, h).start()

        @pl.when(has_next)
        def _():
            r_copy(1, h).start()

        for e in range(1, n_sa):
            g_copy(h, e).start()
        y_start(2, h)
        y_start(3, h)

        @pl.when(h >= LAG)
        def _():
            finish(h - LAG)

        return c

    lax.fori_loop(0, heads, step, 0)

    def tail(h, c):
        finish(h)
        return c

    lax.fori_loop(max(heads - LAG, 0), heads, tail, 0)

    def close(h, c):
        for kind in range(4):
            for d in range(1, n_wa):
                x_copy(kind, h, d, w).wait_send()
                y_copy(kind, h, d, w).wait_send()
                y_copy(kind, h, d, lax.rem(w + n_wa - d, n_wa)).wait_recv()
            y_local(kind, h).wait()
        for e in range(1, n_sa):
            for kind in range(2):
                t_copy(kind, h, e, s).wait_send()
            g_copy(h, e).wait_send()
        for d in range(1, n_wa):
            f_copy(h, d, w).wait_send()
            f_copy(h, d, lax.rem(w + n_wa - d, n_wa)).wait_recv()

        @pl.when(has_next)
        def _():
            z_copy(0, h).wait_send()
            r_copy(1, h).wait_send()

        @pl.when(has_prev)
        def _():
            z_copy(1, h).wait_send()
            r_copy(0, h).wait_send()

        for source in range(n_wa):
            dtk_out[:, cols(source, h)] = t_fin[source, h, 0].astype(F32)
            dtv_out[:, cols(source, h)] = t_fin[source, h, 1].astype(F32)
        return c

    lax.fori_loop(0, heads, close, 0)


def shards(queries, keys, values, text_keys, text_values, out_grad, window_ext):
    n_sa, n_wa = lax.axis_size("sa"), lax.axis_size("wa")
    grid = queries.shape
    channels = grid[-1]
    cells = grid[0] * grid[1] * grid[2]
    heads = channels // HEAD_DIM // n_wa
    text_rows = text_keys.shape[0]
    slab, text = n_wa * cells, n_sa * text_rows
    n_keys = 3 * slab + text
    q_block = min(slab, 256)
    flat = (cells, channels)
    dma = pltpu.SemaphoreType.DMA
    anywhere = pl.BlockSpec(memory_space=pl.ANY)
    in_vmem = pl.BlockSpec(memory_space=pltpu.VMEM)
    cell_out = jax.ShapeDtypeStruct(flat, BF16)
    text_out = jax.ShapeDtypeStruct((text_rows, channels), F32)
    outs = pl.pallas_call(
        functools.partial(kernel, n_sa, n_wa, heads, cells, text_rows),
        out_shape=(cell_out,) * 4 + (text_out,) * 2,
        in_specs=[pl.BlockSpec(memory_space=pltpu.SMEM)] + [anywhere] * 6,
        out_specs=(anywhere,) * 4 + (in_vmem,) * 2,
        scratch_shapes=[
            pltpu.VMEM((heads, 2, n_keys, HEAD_DIM), BF16),
            pltpu.VMEM((heads, 2, slab, HEAD_DIM), BF16),
            pltpu.VMEM((heads, 2, slab, HEAD_DIM), BF16),
            pltpu.VMEM((heads, 2, slab, HEAD_DIM), F32),
            pltpu.VMEM((2, heads, 2, slab, HEAD_DIM), BF16),
            pltpu.VMEM((2, heads, 2, slab, HEAD_DIM), BF16),
            pltpu.VMEM((heads, 2, slab, HEAD_DIM), BF16),
            pltpu.VMEM((heads, 2, text, HEAD_DIM), BF16),
            pltpu.VMEM((n_sa - 1, heads, 2, text_rows, HEAD_DIM), BF16),
            pltpu.VMEM((n_wa, heads, 2, text_rows, HEAD_DIM), BF16),
            pltpu.VMEM((n_keys, q_block), F32),
            pltpu.VMEM((n_keys, q_block), BF16),
            pltpu.VMEM((n_keys, q_block), BF16),
            dma((n_wa - 1, heads, 4)),
            dma((n_wa - 1, heads, 4)),
            dma((heads, 4)),
            dma((n_sa - 1, heads, 2)),
            dma((n_sa - 1, heads, 2)),
            dma((heads, 2)),
            dma((2, heads)),
            dma((2, heads)),
            dma((2, heads)),
            dma((2, heads)),
            dma((n_wa - 1, heads, 4)),
            dma((n_wa - 1, heads, 4)),
            dma((heads, 4)),
            dma((n_sa - 1, heads)),
            dma((n_sa - 1, heads)),
            dma((n_wa - 1, heads)),
            dma((n_wa - 1, heads)),
        ],
        compiler_params=pltpu.CompilerParams(
            collective_id=0, has_side_effects=True, vmem_limit_bytes=60 * 1024 * 1024
        ),
    )(
        window_ext, queries.reshape(flat), keys.reshape(flat), values.reshape(flat),
        out_grad.reshape(flat), text_keys, text_values,
    )
    return tuple(out.reshape(grid) for out in outs[:4]) + tuple(outs[4:])


def solution(mesh):
    cell = P(("clips", "sa"), None, "wa", "hp")
    text = P(("clips", "sa"), "hp")
    return jax.shard_map(
        shards,
        mesh=mesh,
        in_specs=(cell, cell, cell, text, text, cell, P("hp", None)),
        out_specs=(cell, cell, cell, cell, text, text),
        check_vma=False,
    )
```

```python
import functools

import jax
import jax.numpy as jnp
from jax import lax
from jax.experimental import pallas as pl
from jax.experimental.pallas import tpu as pltpu
from jax.sharding import PartitionSpec as P

HEAD_DIM = 128
NEG = -1e30
MESH = pl.DeviceIdType.MESH
F32 = jnp.float32
BF16 = jnp.bfloat16
KEY_BLOCK = 256
LOOKAHEAD = 3
LAG = 2


def dot_nt(a, b):
    return lax.dot_general(a, b, (((1,), (1,)), ((), ())), preferred_element_type=F32)


def dot_tn(a, b):
    return lax.dot_general(a, b, (((0,), (0,)), ((), ())), preferred_element_type=F32)


def kernel(
    n_sa, n_wa, heads, cells, text_rows,
    window, q_in, k_in, v_in, g_in, tk_in, tv_in,
    o_out, dq_out, dk_out, dv_out, dtk_out, dtv_out,
    kv, qg, oq, own_part, z_part, z_got, fin, t_part, t_got, t_fin, st, wb, db,
    x_send, x_recv, x_loc, t_send, t_recv, t_loc, z_send, z_recv,
    r_send, r_recv, y_send, y_recv, y_loc, g_send, g_recv, f_send, f_recv,
):
    s = lax.axis_index("sa")
    w = lax.axis_index("wa")
    slab = n_wa * cells
    text = n_sa * text_rows
    text_base = 3 * slab
    n_keys = text_base + text
    scale = HEAD_DIM ** (-0.5)
    has_prev, has_next = s > 0, s < n_sa - 1
    before, after = lax.rem(s + n_sa - 1, n_sa), lax.rem(s + 1, n_sa)

    def cols(group, h):
        return pl.ds(pl.multiple_of((group * heads + h) * HEAD_DIM, HEAD_DIM), HEAD_DIM)

    def rows_of(base, index, size):
        return pl.ds(pl.multiple_of(base + index * size, 16), size)

    def remote(src, dst, send, recv, **where):
        return pltpu.make_async_remote_copy(
            src_ref=src, dst_ref=dst, send_sem=send, recv_sem=recv,
            device_id=where, device_id_type=MESH,
        )

    barrier = pltpu.get_barrier_semaphore()
    for d in range(1, n_wa):
        pl.semaphore_signal(barrier, inc=1, device_id={"wa": lax.rem(w + d, n_wa)}, device_id_type=MESH)
    neighbours = n_wa - 1 + has_prev.astype(jnp.int32) + has_next.astype(jnp.int32)

    @pl.when(has_prev)
    def _():
        pl.semaphore_signal(barrier, inc=1, device_id={"sa": before}, device_id_type=MESH)

    @pl.when(has_next)
    def _():
        pl.semaphore_signal(barrier, inc=1, device_id={"sa": after}, device_id_type=MESH)

    pl.semaphore_wait(barrier, neighbours)

    ins = (k_in, v_in, q_in, g_in)

    def x_slot(kind, h, source):
        if kind < 2:
            return kv.at[h, kind, rows_of(slab, source, cells)]
        return qg.at[h, kind - 2, rows_of(0, source, cells)]

    def x_copy(kind, h, d, source):
        peer = lax.rem(w + d, n_wa)
        return remote(
            ins[kind].at[:, cols(peer, h)], x_slot(kind, h, source),
            x_send.at[d - 1, h, kind], x_recv.at[d - 1, h, kind], wa=peer,
        )

    def x_local(kind, h):
        return pltpu.make_async_copy(ins[kind].at[:, cols(w, h)], x_slot(kind, h, w), x_loc.at[h, kind])

    def x_wait(kind, h):
        x_local(kind, h).wait()
        for d in range(1, n_wa):
            x_copy(kind, h, d, lax.rem(w + n_wa - d, n_wa)).wait_recv()

    texts = (tk_in, tv_in)

    def t_slot(h, block):
        return kv.at[h, :, rows_of(text_base, block, text_rows)]

    def t_hop(side, h, hop, block):
        return remote(
            t_slot(h, block), t_slot(h, block), t_send.at[side, h, hop], t_recv.at[side, h, hop],
            sa=after if side == 0 else before,
        )

    def t_out(side, h, hop):
        return t_hop(side, h, hop, s - hop if side == 0 else s + hop)

    def t_in(side, h, hop):
        return t_hop(side, h, hop, s - 1 - hop if side == 0 else s + 1 + hop)

    def t_valid(side, hop):
        if side == 0:
            return jnp.logical_and(s >= hop, has_next)
        return jnp.logical_and(s + hop < n_sa, has_prev)

    def t_local(kind, h):
        return pltpu.make_async_copy(
            texts[kind].at[:, cols(w, h)],
            kv.at[h, kind, rows_of(text_base, s, text_rows)], t_loc.at[h, kind],
        )

    def t_forward(h, hop):
        for side in range(2):
            @pl.when(t_valid(side, hop))
            def _():
                if hop:
                    t_in(side, h, hop - 1).wait_recv()
                t_out(side, h, hop).start()

    def z_copy(side, h):
        target = lax.rem(s + 1, n_sa) if side == 0 else lax.rem(s + n_sa - 1, n_sa)
        return remote(
            kv.at[h, :, pl.ds(slab, slab)], kv.at[h, :, pl.ds(0 if side == 0 else 2 * slab, slab)],
            z_send.at[side, h], z_recv.at[side, h], sa=target,
        )

    def r_copy(side, h):
        target = lax.rem(s + n_sa - 1, n_sa) if side == 0 else lax.rem(s + 1, n_sa)
        return remote(
            z_part.at[side, h], z_got.at[side, h], r_send.at[side, h], r_recv.at[side, h], sa=target,
        )

    @pl.when(jnp.logical_not(has_prev))
    def _():
        def clear(h, c):
            kv[h, :, pl.ds(0, slab)] = jnp.zeros((2, slab, HEAD_DIM), BF16)
            z_got[1, h] = jnp.zeros((2, slab, HEAD_DIM), BF16)
            t_got[0, h, 0] = jnp.zeros((2, text_rows, HEAD_DIM), BF16)
            return c

        lax.fori_loop(0, heads, clear, 0)

    @pl.when(jnp.logical_not(has_next))
    def _():
        def clear(h, c):
            kv[h, :, pl.ds(2 * slab, slab)] = jnp.zeros((2, slab, HEAD_DIM), BF16)
            z_got[0, h] = jnp.zeros((2, slab, HEAD_DIM), BF16)
            t_got[1, h, n_sa - 1] = jnp.zeros((2, text_rows, HEAD_DIM), BF16)
            return c

        lax.fori_loop(0, heads, clear, 0)

    def open_head(h, c):
        for kind in range(4):
            for d in range(1, n_wa):
                x_copy(kind, h, d, w).start()
        for kind in range(2):
            t_local(kind, h).start()
        for kind in range(4):
            x_local(kind, h).start()
        return c

    lax.fori_loop(0, heads, open_head, 0)

    def open_text(h, c):
        for kind in range(2):
            t_local(kind, h).wait()
        t_forward(h, 0)
        return c

    lax.fori_loop(0, heads, open_text, 0)

    def feed(h):
        x_wait(0, h)
        x_wait(1, h)

        @pl.when(has_next)
        def _():
            z_copy(0, h).start()

        @pl.when(has_prev)
        def _():
            z_copy(1, h).start()

        t_forward(h, 1)

    def feed_text(h):
        for hop in range(2, n_sa - 1):
            t_forward(h, hop)

    for h in range(min(LOOKAHEAD, heads)):
        feed(h)
    for h in range(min(LOOKAHEAD - 1, heads)):
        feed_text(h)

    q_block = min(slab, 256)

    def compute(h):
        ext_t = window[0, w * heads + h]
        ext_w = window[2, w * heads + h]
        near = (
            jnp.logical_and(has_prev, ext_t >= 1),
            None,
            jnp.logical_and(has_next, ext_t >= 1),
        )
        for qb in range(slab // q_block):
            q_rows = pl.ds(qb * q_block, q_block)
            q = qg[h, 0, q_rows]
            g = qg[h, 1, q_rows]
            query_col = qb * (q_block // cells) + lax.broadcasted_iota(jnp.int32, (1, q_block), 1) // cells
            top = jnp.full((1, q_block), NEG, F32)
            blocks = []
            for j in range(3):
                far = 0.0 if near[j] is None else jnp.where(near[j], 0.0, NEG)
                for c in range(n_wa):
                    bias = jnp.where(jnp.abs(query_col - c) <= ext_w, far, NEG)
                    blocks.append(((j * n_wa + c) * cells, cells, bias))
            for b in range(0, text, KEY_BLOCK):
                blocks.append((text_base + b, min(KEY_BLOCK, text - b), None))
            for start, size, bias in blocks:
                sc = dot_nt(kv[h, 0, pl.ds(start, size)], q) * scale
                if bias is not None:
                    sc = sc + bias
                st[pl.ds(start, size)] = sc
                top = jnp.maximum(top, jnp.max(sc, axis=0, keepdims=True))
            total = jnp.zeros((1, q_block), F32)
            for start, size, _ in blocks:
                p = jnp.exp(st[pl.ds(start, size)] - top)
                st[pl.ds(start, size)] = p
                total = total + jnp.sum(p, axis=0, keepdims=True)
            inv = 1.0 / total
            for start, size, _ in blocks:
                wb[pl.ds(start, size)] = (st[pl.ds(start, size)] * inv).astype(BF16)
            attended = dot_tn(wb[...], kv[h, 1]).astype(BF16)
            oq[h, 0, q_rows] = attended
            product = g.astype(F32) * attended.astype(F32)
            delta = jnp.sum(product.T, axis=0, keepdims=True)
            inv_scale = inv * scale
            for start, size, _ in blocks:
                dp = dot_nt(kv[h, 1, pl.ds(start, size)], g)
                db[pl.ds(start, size)] = (st[pl.ds(start, size)] * inv_scale * (dp - delta)).astype(BF16)
            oq[h, 1, q_rows] = dot_tn(db[...], kv[h, 0]).astype(BF16)

            def put(ref, index, value, at):
                if qb == 0:
                    ref[index] = value.astype(ref.dtype)
                else:
                    ref[index] = (ref[index].astype(F32) + value).astype(ref.dtype)

            for kind, (left, right) in enumerate(((db, q), (wb, g))):
                for j in range(3):
                    part = jnp.dot(left[pl.ds(j * slab, slab)], right, preferred_element_type=F32)
                    if j == 1:
                        put(own_part, (h, kind), part, qb)
                    else:
                        put(z_part, (j // 2, h, kind), part, qb)
                part = jnp.dot(left[pl.ds(text_base, text)], right, preferred_element_type=F32)
                put(t_part, (h, kind), part, qb)

    outs = (dk_out, dv_out, o_out, dq_out)

    def y_src(kind, h, owner):
        ref = fin if kind < 2 else oq
        return ref.at[h, kind % 2, rows_of(0, owner, cells)]

    def y_copy(kind, h, d, source):
        peer = lax.rem(w + d, n_wa)
        return remote(
            y_src(kind, h, peer), outs[kind].at[:, cols(source, h)],
            y_send.at[d - 1, h, kind], y_recv.at[d - 1, h, kind], wa=peer,
        )

    def y_local(kind, h):
        return pltpu.make_async_copy(y_src(kind, h, w), outs[kind].at[:, cols(w, h)], y_loc.at[h, kind])

    def y_start(kind, h):
        for d in range(1, n_wa):
            y_copy(kind, h, d, w).start()
        y_local(kind, h).start()

    def g_copy(side, h, block):
        return remote(
            t_part.at[h, :, rows_of(0, block, text_rows)], t_got.at[side, h, block],
            g_send.at[side, h, block], g_recv.at[side, h, block],
            sa=after if side == 0 else before,
        )

    def g_valid(side, block):
        return s < block if side == 0 else s > block

    def g_relay(side, h):
        inward = has_prev if side == 0 else has_next
        for block in range(n_sa):
            @pl.when(g_valid(side, block))
            def _():
                @pl.when(inward)
                def _():
                    g_copy(side, h, block).wait_recv()
                    rows = pl.ds(block * text_rows, text_rows)
                    joined = t_part[h, :, rows].astype(F32) + t_got[side, h, block].astype(F32)
                    t_part[h, :, rows] = joined.astype(BF16)

                g_copy(side, h, block).start()

    def f_copy(h, d, source):
        return remote(
            t_fin.at[w, h], t_fin.at[source, h],
            f_send.at[d - 1, h], f_recv.at[d - 1, h], wa=lax.rem(w + d, n_wa),
        )

    def finish(h):
        @pl.when(has_next)
        def _():
            r_copy(0, h).wait_recv()

        @pl.when(has_prev)
        def _():
            r_copy(1, h).wait_recv()

        whole = own_part[h] + z_got[0, h].astype(F32) + z_got[1, h].astype(F32)
        fin[h] = whole.astype(BF16)
        y_start(0, h)
        y_start(1, h)

    def finish_text(h):
        @pl.when(has_prev)
        def _():
            g_copy(0, h, s).wait_recv()

        @pl.when(has_next)
        def _():
            g_copy(1, h, s).wait_recv()

        whole = t_part[h, :, rows_of(0, s, text_rows)].astype(F32)
        whole = whole + t_got[0, h, s].astype(F32) + t_got[1, h, s].astype(F32)
        t_fin[w, h] = whole.astype(BF16)
        for d in range(1, n_wa):
            f_copy(h, d, w).start()

    def attend(h):
        x_wait(2, h)
        x_wait(3, h)

        @pl.when(jnp.logical_not(has_next))
        def _():
            for hop in range(n_sa - 1):
                t_in(0, h, hop).wait_recv()

        @pl.when(jnp.logical_not(has_prev))
        def _():
            for hop in range(n_sa - 1):
                t_in(1, h, hop).wait_recv()

        @pl.when(has_prev)
        def _():
            z_copy(0, h).wait_recv()

        @pl.when(has_next)
        def _():
            z_copy(1, h).wait_recv()

        compute(h)

        @pl.when(has_prev)
        def _():
            r_copy(0, h).start()

        @pl.when(has_next)
        def _():
            r_copy(1, h).start()

        y_start(2, h)
        y_start(3, h)

    def step(i, c):
        @pl.when(i + LOOKAHEAD < heads)
        def _():
            feed(i + LOOKAHEAD)

        @pl.when(i + LOOKAHEAD - 1 < heads)
        def _():
            feed_text(i + LOOKAHEAD - 1)

        @pl.when(i < heads)
        def _():
            attend(i)

        for side in range(2):
            h = i - (s if side == 0 else n_sa - 1 - s)

            @pl.when(jnp.logical_and(h >= 0, h < heads))
            def _():
                g_relay(side, h)

        @pl.when(jnp.logical_and(i >= LAG, i < heads + LAG))
        def _():
            finish(i - LAG)

        @pl.when(jnp.logical_and(i >= n_sa - 1, i < heads + n_sa - 1))
        def _():
            finish_text(i - (n_sa - 1))

        return c

    lax.fori_loop(0, heads + max(n_sa - 1, LAG), step, 0)

    def close(h, c):
        for kind in range(4):
            for d in range(1, n_wa):
                x_copy(kind, h, d, w).wait_send()
                y_copy(kind, h, d, w).wait_send()
                y_copy(kind, h, d, lax.rem(w + n_wa - d, n_wa)).wait_recv()
            y_local(kind, h).wait()
        for side in range(2):
            for hop in range(n_sa - 1):
                @pl.when(t_valid(side, hop))
                def _():
                    t_out(side, h, hop).wait_send()

            for block in range(n_sa):
                @pl.when(g_valid(side, block))
                def _():
                    g_copy(side, h, block).wait_send()

        for d in range(1, n_wa):
            f_copy(h, d, w).wait_send()
            f_copy(h, d, lax.rem(w + n_wa - d, n_wa)).wait_recv()

        @pl.when(has_next)
        def _():
            z_copy(0, h).wait_send()
            r_copy(1, h).wait_send()

        @pl.when(has_prev)
        def _():
            z_copy(1, h).wait_send()
            r_copy(0, h).wait_send()

        for source in range(n_wa):
            dtk_out[:, cols(source, h)] = t_fin[source, h, 0]
            dtv_out[:, cols(source, h)] = t_fin[source, h, 1]
        return c

    lax.fori_loop(0, heads, close, 0)


def hand_over(*refs):
    half = len(refs) // 2
    for source, target in zip(refs[:half], refs[half:]):
        target[...] = source[...].astype(target.dtype)


def shards(queries, keys, values, text_keys, text_values, out_grad, window_ext):
    n_sa, n_wa = lax.axis_size("sa"), lax.axis_size("wa")
    grid = queries.shape
    channels = grid[-1]
    cells = grid[0] * grid[1] * grid[2]
    heads = channels // HEAD_DIM // n_wa
    text_rows = text_keys.shape[0]
    slab, text = n_wa * cells, n_sa * text_rows
    n_keys = 3 * slab + text
    q_block = min(slab, 256)
    flat = (cells, channels)
    dma = pltpu.SemaphoreType.DMA
    anywhere = pl.BlockSpec(memory_space=pl.ANY)
    in_vmem = pl.BlockSpec(memory_space=pltpu.VMEM)
    cell_out = jax.ShapeDtypeStruct(flat, BF16)
    text_out = jax.ShapeDtypeStruct((text_rows, channels), BF16)
    outs = pl.pallas_call(
        functools.partial(kernel, n_sa, n_wa, heads, cells, text_rows),
        out_shape=(cell_out,) * 4 + (text_out,) * 2,
        in_specs=[pl.BlockSpec(memory_space=pltpu.SMEM)] + [anywhere] * 6,
        out_specs=(anywhere,) * 4 + (in_vmem,) * 2,
        scratch_shapes=[
            pltpu.VMEM((heads, 2, n_keys, HEAD_DIM), BF16),
            pltpu.VMEM((heads, 2, slab, HEAD_DIM), BF16),
            pltpu.VMEM((heads, 2, slab, HEAD_DIM), BF16),
            pltpu.VMEM((heads, 2, slab, HEAD_DIM), F32),
            pltpu.VMEM((2, heads, 2, slab, HEAD_DIM), BF16),
            pltpu.VMEM((2, heads, 2, slab, HEAD_DIM), BF16),
            pltpu.VMEM((heads, 2, slab, HEAD_DIM), BF16),
            pltpu.VMEM((heads, 2, text, HEAD_DIM), BF16),
            pltpu.VMEM((2, heads, n_sa, 2, text_rows, HEAD_DIM), BF16),
            pltpu.VMEM((n_wa, heads, 2, text_rows, HEAD_DIM), BF16),
            pltpu.VMEM((n_keys, q_block), F32),
            pltpu.VMEM((n_keys, q_block), BF16),
            pltpu.VMEM((n_keys, q_block), BF16),
            dma((n_wa - 1, heads, 4)),
            dma((n_wa - 1, heads, 4)),
            dma((heads, 4)),
            dma((2, heads, n_sa - 1)),
            dma((2, heads, n_sa - 1)),
            dma((heads, 2)),
            dma((2, heads)),
            dma((2, heads)),
            dma((2, heads)),
            dma((2, heads)),
            dma((n_wa - 1, heads, 4)),
            dma((n_wa - 1, heads, 4)),
            dma((heads, 4)),
            dma((2, heads, n_sa)),
            dma((2, heads, n_sa)),
            dma((n_wa - 1, heads)),
            dma((n_wa - 1, heads)),
        ],
        compiler_params=pltpu.CompilerParams(
            collective_id=0, has_side_effects=True, vmem_limit_bytes=60 * 1024 * 1024
        ),
    )(
        window_ext.T, queries.reshape(flat), keys.reshape(flat), values.reshape(flat),
        out_grad.reshape(flat), text_keys, text_values,
    )
    text_sum = jax.ShapeDtypeStruct((text_rows, channels), F32)
    outs = pl.pallas_call(
        hand_over,
        out_shape=(cell_out,) * 4 + (text_sum,) * 2,
        in_specs=[in_vmem] * 6,
        out_specs=(in_vmem,) * 6,
    )(*outs)
    return tuple(out.reshape(grid) for out in outs[:4]) + tuple(outs[4:])


def solution(mesh):
    cell = P(("clips", "sa"), None, "wa", "hp")
    text = P(("clips", "sa"), "hp")
    return jax.shard_map(
        shards,
        mesh=mesh,
        in_specs=(cell, cell, cell, text, text, cell, P("hp", None)),
        out_specs=(cell, cell, cell, cell, text, text),
        check_vma=False,
    )
```
